32 devices in a mesh: row: 8 (over y, x, core), col: 4 (over z).
Axes of the slice: x: 2, y: 2, z: 4, core: 2. Of those that a mesh axis runs over, the one named last changes fastest.
Arguments:
- amplitudes: float32 [16, 16, 1024, 1024], P(None, None, 'row', 'col'), may hold values from -6 to 6
- hole_ints: float32 [256, 256], replicated, may hold values from -0.375 to 0.375
- factors: bfloat16 [1024, 1024], replicated, may hold values from -0.1875 to 0.1875
- core_matrix: float32 [1024, 1024], replicated, may hold values from -5 to 5
Outputs:
- residual: float32 [16, 16, 1024, 1024], P(None, None, 'row', 'col')
The draws below stay inside these ranges and needn't reach their ends.
All inputs are finite; a program needn't handle non-finite values.
Results may differ from the reference program's by a relative error of at most 0.0046.
Values sent between devices are 32-bit elements; how exact they have to be, the bound alone decides.
A program may use at most 256 MiB of HBM per device.

```python
import jax
import jax.numpy as jnp
from jax import lax

O = 16
V = 1024
NG = 1024
PAIRS = 256


def steps_of(rng, dims, shards, low, top_value):
    gain = 1.0
    for dim, parts in shards:
        draws = jax.random.uniform(jax.random.fold_in(jax.random.fold_in(rng, 6), dim), (parts,), jnp.float32, low / len(shards), top_value / len(shards))
        gain = gain * jnp.repeat(jnp.exp(draws), dims[dim] // parts).reshape((-1,) + (1,) * (len(dims) - 1 - dim))
    return gain


def centred(rng, shape, deviation, bound, split=(), held_as=jnp.bfloat16):
    factor_of = steps_of(rng, shape, split, -0.22, 0.18) if split else 1.0
    entries = jax.random.normal(rng, shape, jnp.float32) * deviation * factor_of
    return jnp.minimum(jnp.maximum(entries, -bound), bound).astype(held_as)


def setup_inputs(seed: int = 0) -> dict:
    key_of = jax.random.split(jax.random.key(seed), 5)
    return {
        "amplitudes": centred(key_of[0], (O, O, V, V), 1.0, 6.0, ((2, 8), (3, 4)), jnp.float32),
        "hole_ints": centred(key_of[1], (PAIRS, PAIRS), PAIRS ** -0.5, 0.375, (), jnp.float32),
        "factors": centred(key_of[2], (V, NG), V ** -0.5, 0.1875),
        "core_matrix": centred(key_of[3], (NG, NG), 1.0, 5.0, (), jnp.float32),
    }


def particle_ladder(matrix, factors, core_matrix):
    rounded = matrix.astype(jnp.bfloat16)
    left_side = jnp.dot(rounded, factors, preferred_element_type=jnp.float32).astype(jnp.bfloat16)
    inner = jnp.dot(factors.T, left_side, preferred_element_type=jnp.float32)
    weighted = (core_matrix * inner).astype(jnp.bfloat16)
    spread = jnp.dot(factors, weighted, preferred_element_type=jnp.float32).astype(jnp.bfloat16)
    return matrix + jnp.dot(spread, factors.T, preferred_element_type=jnp.float32)


def reference(amplitudes, hole_ints, factors, core_matrix):
    flattened = amplitudes.reshape(PAIRS, V * V)
    hole_term = jnp.dot(hole_ints, flattened, precision=lax.Precision.HIGHEST, preferred_element_type=jnp.float32)
    hole_term = hole_term.reshape(O, O, V, V)
    summed = hole_term + jnp.transpose(hole_term, (1, 0, 3, 2))
    summed = summed.reshape(PAIRS, V, V)
    result = lax.map(lambda matrix: particle_ladder(matrix, factors, core_matrix), summed)
    return result.reshape(O, O, V, V)
```

```python
import functools

import jax
import jax.numpy as jnp
import numpy as np
from jax import lax
from jax.experimental import pallas as pl
from jax.experimental.pallas import tpu as pltpu
from jax.sharding import PartitionSpec as P

VMEM_LIMIT = 60 * 1024 * 1024


def couple_order(occupied):
    listing = []
    for first in range(occupied):
        for second in range(first + 1, occupied):
            listing += [first * occupied + second, second * occupied + first]
    listing += [first * occupied + first for first in range(occupied)]
    return np.array(listing, dtype=np.int32)


def hole_kernel(weights_ref, amplitudes_ref, out_ref):
    weights = weights_ref[...]
    slots = weights.shape[0]
    high = weights.astype(jnp.bfloat16)
    low = (weights - high.astype(jnp.float32)).astype(jnp.bfloat16)
    both = jnp.concatenate([high, low], axis=0)
    for row in range(amplitudes_ref.shape[1]):
        values = amplitudes_ref[:, row, :]
        top = values.astype(jnp.bfloat16)
        rest = (values - top.astype(jnp.float32)).astype(jnp.bfloat16)
        main = jnp.dot(both, top, preferred_element_type=jnp.float32)
        small = jnp.dot(high, rest, preferred_element_type=jnp.float32)
        out_ref[:, row, :] = main[:slots] + (main[slots:] + small)


def hole(weights, amplitudes):
    slots, pairs = weights.shape
    _, rows, cols = amplitudes.shape
    step = 8
    return pl.pallas_call(
        hole_kernel,
        grid=(rows // step,),
        in_specs=[
            pl.BlockSpec((slots, pairs), lambda i: (0, 0)),
            pl.BlockSpec((pairs, step, cols), lambda i: (0, i, 0)),
        ],
        out_specs=pl.BlockSpec((slots, step, cols), lambda i: (0, i, 0)),
        out_shape=jax.ShapeDtypeStruct((slots, rows, cols), jnp.float32),
        compiler_params=pltpu.CompilerParams(vmem_limit_bytes=VMEM_LIMIT),
        cost_estimate=pl.CostEstimate(
            flops=6 * slots * pairs * rows * cols,
            bytes_accessed=4 * (slots + pairs) * rows * cols,
            transcendentals=0,
        ),
        name="hole",
    )(weights, amplitudes)


def ladder_kernel(diagonal_ref, blocks_ref, factors_ref, turned_ref, core_ref, out_ref,
                  summed, left, weighted):
    row_count, col_count, _, rows, cols = blocks_ref.shape
    virtual = row_count * rows
    grid_points = factors_ref.shape[1]
    tile = 256
    row_blocks = tile // rows
    col_blocks = tile // cols
    tiles = virtual // tile

    def one(which, _):
        partner = jnp.where(diagonal_ref[0] != 0, which, 1 - which)

        def first(t, _):
            span = pl.ds(pl.multiple_of(t * tile, tile), tile)
            for c in range(tiles):
                straight = jnp.concatenate(
                    [
                        jnp.concatenate(
                            [blocks_ref[t * row_blocks + r, c * col_blocks + q, which] for q in range(col_blocks)],
                            axis=1,
                        )
                        for r in range(row_blocks)
                    ],
                    axis=0,
                )
                other = jnp.concatenate(
                    [
                        jnp.concatenate(
                            [blocks_ref[c * row_blocks + r, t * col_blocks + q, partner] for q in range(col_blocks)],
                            axis=1,
                        )
                        for r in range(row_blocks)
                    ],
                    axis=0,
                )
                summed[span, c * tile:(c + 1) * tile] = straight + other.T
            left[span, :] = jnp.dot(
                summed[span, :].astype(jnp.bfloat16), factors_ref[...], preferred_element_type=jnp.float32
            ).astype(jnp.bfloat16)
            return 0

        lax.fori_loop(0, tiles, first, 0)

        def second(t, _):
            span = pl.ds(pl.multiple_of(t * tile, tile), tile)
            inner = jnp.dot(turned_ref[span, :], left[...], preferred_element_type=jnp.float32)
            weighted[span, :] = (core_ref[span, :] * inner).astype(jnp.bfloat16)
            return 0

        lax.fori_loop(0, grid_points // tile, second, 0)

        def third(t, _):
            span = pl.ds(pl.multiple_of(t * tile, tile), tile)
            spread = jnp.dot(
                factors_ref[span, :], weighted[...], preferred_element_type=jnp.float32
            ).astype(jnp.bfloat16)
            result = summed[span, :] + jnp.dot(spread, turned_ref[...], preferred_element_type=jnp.float32)
            for r in range(row_blocks):
                for c in range(col_count):
                    out_ref[t * row_blocks + r, c, which] = result[r * rows:(r + 1) * rows, c * cols:(c + 1) * cols]
            return 0

        lax.fori_loop(0, tiles, third, 0)
        return 0

    lax.fori_loop(0, 2, one, 0)


def ladder(diagonal, blocks, factors, turned, core_matrix):
    row_count, _, _, rows, _ = blocks.shape
    virtual = row_count * rows
    grid_points = factors.shape[1]
    vmem = pl.BlockSpec(memory_space=pltpu.VMEM)
    return pl.pallas_call(
        ladder_kernel,
        in_specs=[pl.BlockSpec(memory_space=pltpu.SMEM), vmem, vmem, vmem, vmem],
        out_specs=vmem,
        out_shape=jax.ShapeDtypeStruct(blocks.shape, jnp.float32),
        scratch_shapes=[
            pltpu.VMEM((virtual, virtual), jnp.float32),
            pltpu.VMEM((virtual, grid_points), jnp.bfloat16),
            pltpu.VMEM((grid_points, grid_points), jnp.bfloat16),
        ],
        compiler_params=pltpu.CompilerParams(vmem_limit_bytes=VMEM_LIMIT),
        cost_estimate=pl.CostEstimate(
            flops=16 * virtual * virtual * grid_points,
            bytes_accessed=24 * virtual * virtual,
            transcendentals=0,
        ),
        name="ladder",
    )(diagonal, blocks, factors, turned, core_matrix)


def place_kernel(places, group, blocks_ref, *refs):
    out_ref, held, in_sems, out_sems = refs[-4:]
    slots = len(places)

    def fetch(g):
        span = pl.ds(g * group, group)
        return pltpu.make_async_copy(blocks_ref.at[span], held.at[span], in_sems.at[g])

    def put(s):
        return pltpu.make_async_copy(held.at[s], out_ref.at[places[s]], out_sems.at[s])

    for g in range(slots // group):
        fetch(g).start()
    for g in range(slots // group):
        fetch(g).wait()
        for s in range(g * group, (g + 1) * group):
            put(s).start()
    for s in range(slots):
        put(s).wait()


def place(blocks, target, places, pairs):
    slots, rows, cols = blocks.shape
    group = max(1, slots // 8)
    hbm = pl.BlockSpec(memory_space=pl.ANY)
    operands = (blocks,) if target is None else (blocks, target)
    return pl.pallas_call(
        functools.partial(place_kernel, [int(p) for p in places], group),
        in_specs=[hbm] * len(operands),
        out_specs=hbm,
        out_shape=jax.ShapeDtypeStruct((pairs, rows, cols), jnp.float32),
        scratch_shapes=[
            pltpu.VMEM((slots, rows, cols), jnp.float32),
            pltpu.SemaphoreType.DMA((slots // group,)),
            pltpu.SemaphoreType.DMA((slots,)),
        ],
        input_output_aliases={} if target is None else {1: 0},
        compiler_params=pltpu.CompilerParams(vmem_limit_bytes=VMEM_LIMIT),
        cost_estimate=pl.CostEstimate(flops=0, bytes_accessed=8 * slots * rows * cols, transcendentals=0),
        name="place",
    )(*operands)


def exchange(blocks):
    return lax.all_to_all(blocks, ("row", "col"), split_axis=0, concat_axis=0, tiled=True)


def local(amplitudes, hole_ints, factors, core_matrix):
    row_count = lax.axis_size("row")
    col_count = lax.axis_size("col")
    devices = row_count * col_count
    occupied, _, rows, cols = amplitudes.shape
    pairs = occupied * occupied
    chunks = pairs // (2 * devices)
    slots = 2 * devices
    flattened = amplitudes.reshape(pairs, rows, cols)
    order = couple_order(occupied)
    weights = jnp.take(hole_ints, jnp.asarray(order), axis=0)
    turned = factors.T
    me = lax.axis_index(("row", "col"))
    first_diagonal = occupied * (occupied - 1) // 2

    arrived = []
    for k in range(chunks):
        term = hole(weights[k * slots:(k + 1) * slots], flattened)
        arrived.append(exchange(term.reshape(devices, 2, rows, cols)))
    returned = []
    for k in range(chunks):
        blocks = arrived[k].reshape(row_count, col_count, 2, rows, cols)
        diagonal = (k * devices + me >= first_diagonal).astype(jnp.int32).reshape(1)
        result = ladder(diagonal, blocks, factors, turned, core_matrix)
        returned.append(exchange(result.reshape(devices, 2, rows, cols)))
    residual = None
    for k in range(chunks):
        residual = place(
            returned[k].reshape(slots, rows, cols), residual, order[k * slots:(k + 1) * slots], pairs
        )
    return residual.reshape(amplitudes.shape)


def solution(mesh):
    return jax.shard_map(
        local,
        mesh=mesh,
        in_specs=(P(None, None, "row", "col"), P(), P(), P()),
        out_specs=P(None, None, "row", "col"),
        check_vma=False,
    )
```

```python
import functools

import jax
import jax.numpy as jnp
import numpy as np
from jax import lax
from jax.experimental import pallas as pl
from jax.experimental.pallas import tpu as pltpu
from jax.sharding import PartitionSpec as P

VMEM_LIMIT = 60 * 1024 * 1024


def couple_order(occupied):
    listing = []
    for first in range(occupied):
        for second in range(first + 1, occupied):
            listing += [first * occupied + second, second * occupied + first]
    listing += [first * occupied + first for first in range(occupied)]
    return np.array(listing, dtype=np.int32)


def hole_kernel(weights_ref, amplitudes_ref, out_ref):
    weights = weights_ref[...]
    slots = weights.shape[0]
    high = weights.astype(jnp.bfloat16)
    low = (weights - high.astype(jnp.float32)).astype(jnp.bfloat16)
    both = jnp.concatenate([high, low], axis=0)
    by_row = jnp.swapaxes(amplitudes_ref[...], 0, 1)
    terms = []
    for row in range(by_row.shape[0]):
        values = by_row[row]
        top = values.astype(jnp.bfloat16)
        rest = (values - top.astype(jnp.float32)).astype(jnp.bfloat16)
        main = jnp.dot(both, top, preferred_element_type=jnp.float32)
        small = jnp.dot(high, rest, preferred_element_type=jnp.float32)
        terms.append(main[:slots] + (main[slots:] + small))
    out_ref[...] = jnp.swapaxes(jnp.stack(terms, axis=0), 0, 1)


def hole(weights, amplitudes):
    slots, pairs = weights.shape
    _, rows, cols = amplitudes.shape
    step = 8
    return pl.pallas_call(
        hole_kernel,
        grid=(rows // step,),
        in_specs=[
            pl.BlockSpec((slots, pairs), lambda i: (0, 0)),
            pl.BlockSpec((pairs, step, cols), lambda i: (0, i, 0)),
        ],
        out_specs=pl.BlockSpec((slots, step, cols), lambda i: (0, i, 0)),
        out_shape=jax.ShapeDtypeStruct((slots, rows, cols), jnp.float32),
        compiler_params=pltpu.CompilerParams(vmem_limit_bytes=VMEM_LIMIT),
        cost_estimate=pl.CostEstimate(
            flops=6 * slots * pairs * rows * cols,
            bytes_accessed=4 * (slots + pairs) * rows * cols,
            transcendentals=0,
        ),
        name="hole",
    )(weights, amplitudes)


def ladder_kernel(diagonal_ref, blocks_ref, factors_ref, turned_ref, core_ref, out_ref,
                  summed, left, weighted):
    row_count, col_count, _, rows, cols = blocks_ref.shape
    virtual = row_count * rows
    grid_points = factors_ref.shape[1]
    tile = 256
    row_blocks = tile // rows
    col_blocks = tile // cols
    tiles = virtual // tile

    def one(which, _):
        partner = jnp.where(diagonal_ref[0] != 0, which, 1 - which)

        def first(t, _):
            span = pl.ds(pl.multiple_of(t * tile, tile), tile)
            for c in range(tiles):
                straight = jnp.concatenate(
                    [
                        jnp.concatenate(
                            [blocks_ref[t * row_blocks + r, c * col_blocks + q, which] for q in range(col_blocks)],
                            axis=1,
                        )
                        for r in range(row_blocks)
                    ],
                    axis=0,
                )
                other = jnp.concatenate(
                    [
                        jnp.concatenate(
                            [blocks_ref[c * row_blocks + r, t * col_blocks + q, partner] for q in range(col_blocks)],
                            axis=1,
                        )
                        for r in range(row_blocks)
                    ],
                    axis=0,
                )
                summed[span, c * tile:(c + 1) * tile] = straight + other.T
            left[span, :] = jnp.dot(
                summed[span, :].astype(jnp.bfloat16), factors_ref[...], preferred_element_type=jnp.float32
            ).astype(jnp.bfloat16)
            return 0

        lax.fori_loop(0, tiles, first, 0)

        def second(t, _):
            span = pl.ds(pl.multiple_of(t * tile, tile), tile)
            inner = jnp.dot(turned_ref[span, :], left[...], preferred_element_type=jnp.float32)
            weighted[span, :] = (core_ref[span, :] * inner).astype(jnp.bfloat16)
            return 0

        lax.fori_loop(0, grid_points // tile, second, 0)

        def third(t, _):
            span = pl.ds(pl.multiple_of(t * tile, tile), tile)
            spread = jnp.dot(
                factors_ref[span, :], weighted[...], preferred_element_type=jnp.float32
            ).astype(jnp.bfloat16)
            result = summed[span, :] + jnp.dot(spread, turned_ref[...], preferred_element_type=jnp.float32)
            for r in range(row_blocks):
                for c in range(col_count):
                    out_ref[t * row_blocks + r, c, which] = result[r * rows:(r + 1) * rows, c * cols:(c + 1) * cols]
            return 0

        lax.fori_loop(0, tiles, third, 0)
        return 0

    lax.fori_loop(0, 2, one, 0)


def ladder(diagonal, blocks, factors, turned, core_matrix):
    row_count, _, _, rows, _ = blocks.shape
    virtual = row_count * rows
    grid_points = factors.shape[1]
    vmem = pl.BlockSpec(memory_space=pltpu.VMEM)
    return pl.pallas_call(
        ladder_kernel,
        in_specs=[pl.BlockSpec(memory_space=pltpu.SMEM), vmem, vmem, vmem, vmem],
        out_specs=vmem,
        out_shape=jax.ShapeDtypeStruct(blocks.shape, jnp.float32),
        scratch_shapes=[
            pltpu.VMEM((virtual, virtual), jnp.float32),
            pltpu.VMEM((virtual, grid_points), jnp.bfloat16),
            pltpu.VMEM((grid_points, grid_points), jnp.bfloat16),
        ],
        compiler_params=pltpu.CompilerParams(vmem_limit_bytes=VMEM_LIMIT),
        cost_estimate=pl.CostEstimate(
            flops=16 * virtual * virtual * grid_points,
            bytes_accessed=24 * virtual * virtual,
            transcendentals=0,
        ),
        name="ladder",
    )(diagonal, blocks, factors, turned, core_matrix)


def place_kernel(places, group, blocks_ref, *refs):
    out_ref, held, in_sems, out_sems = refs[-4:]
    slots = len(places)

    def fetch(g):
        span = pl.ds(g * group, group)
        return pltpu.make_async_copy(blocks_ref.at[span], held.at[span], in_sems.at[g])

    def put(s):
        return pltpu.make_async_copy(held.at[s], out_ref.at[places[s]], out_sems.at[s])

    for g in range(slots // group):
        fetch(g).start()
    for g in range(slots // group):
        fetch(g).wait()
        for s in range(g * group, (g + 1) * group):
            put(s).start()
    for s in range(slots):
        put(s).wait()


def place(blocks, target, places, pairs):
    slots, rows, cols = blocks.shape
    group = max(1, slots // 8)
    hbm = pl.BlockSpec(memory_space=pl.ANY)
    operands = (blocks,) if target is None else (blocks, target)
    return pl.pallas_call(
        functools.partial(place_kernel, [int(p) for p in places], group),
        in_specs=[hbm] * len(operands),
        out_specs=hbm,
        out_shape=jax.ShapeDtypeStruct((pairs, rows, cols), jnp.float32),
        scratch_shapes=[
            pltpu.VMEM((slots, rows, cols), jnp.float32),
            pltpu.SemaphoreType.DMA((slots // group,)),
            pltpu.SemaphoreType.DMA((slots,)),
        ],
        input_output_aliases={} if target is None else {1: 0},
        compiler_params=pltpu.CompilerParams(vmem_limit_bytes=VMEM_LIMIT),
        cost_estimate=pl.CostEstimate(flops=0, bytes_accessed=8 * slots * rows * cols, transcendentals=0),
        name="place",
    )(*operands)


def exchange(blocks):
    return lax.all_to_all(blocks, ("row", "col"), split_axis=0, concat_axis=0, tiled=True)


def local(amplitudes, hole_ints, factors, core_matrix):
    row_count = lax.axis_size("row")
    col_count = lax.axis_size("col")
    devices = row_count * col_count
    occupied, _, rows, cols = amplitudes.shape
    pairs = occupied * occupied
    chunks = pairs // (2 * devices)
    slots = 2 * devices
    flattened = amplitudes.reshape(pairs, rows, cols)
    order = couple_order(occupied)
    weights = jnp.take(hole_ints, jnp.asarray(order), axis=0)
    turned = factors.T
    me = lax.axis_index(("row", "col"))
    first_diagonal = occupied * (occupied - 1) // 2

    arrived = []
    for k in range(chunks):
        term = hole(weights[k * slots:(k + 1) * slots], flattened)
        arrived.append(exchange(term.reshape(devices, 2, rows, cols)))
    returned = []
    for k in range(chunks):
        blocks = arrived[k].reshape(row_count, col_count, 2, rows, cols)
        diagonal = (k * devices + me >= first_diagonal).astype(jnp.int32).reshape(1)
        result = ladder(diagonal, blocks, factors, turned, core_matrix)
        returned.append(exchange(result.reshape(devices, 2, rows, cols)))
    residual = None
    for k in range(chunks):
        residual = place(
            returned[k].reshape(slots, rows, cols), residual, order[k * slots:(k + 1) * slots], pairs
        )
    return residual.reshape(amplitudes.shape)


def solution(mesh):
    return jax.shard_map(
        local,
        mesh=mesh,
        in_specs=(P(None, None, "row", "col"), P(), P(), P()),
        out_specs=P(None, None, "row", "col"),
        check_vma=False,
    )
```
